32 devices in a mesh: ma: 8 (over z, y), sa: 4 (over x, core).
Axes of the slice: x: 2, y: 2, z: 4, core: 2. Of those that a mesh axis runs over, the one named last changes fastest.
Arguments:
- initial_heat_matrix: float32 [128, 128, 8192], P('ma', 'sa'), may hold values from -6 to 6
- conductivity: float32 [128, 8192], P('sa'), may hold values from 0.5 to 2
- laser_x: int32 [128, 2], P('ma'), may hold values from 0 to 127
- laser_y: int32 [128, 2], P('ma'), may hold values from 0 to 127
- pixel_cell: int32 [128, 512], P('sa', 'ma'), may hold values from 0 to 127, as said below
- observed: float32 [128, 512], P('sa', 'ma'), may hold values from -6 to 6
- obs_var: float32 [128, 512], P('sa', 'ma'), may hold values from 20 to 400
Outputs:
- analysis: float32 [128, 128, 8192], P('ma', 'sa')
The draws below stay inside these ranges and needn't reach their ends.
Inputs may be any that keep to these rules, and one draw needn't show every extreme that they name: `pixel_cell`: pixel column j views a surface cell y of its own plane; y lies within 2 of j // 4 and in the same aligned group of 16 cells as that value.
All inputs are finite; a program needn't handle non-finite values.
Results may differ from the reference program's by a relative error of at most 0.000096.
Values sent between devices are 32-bit elements; how exact they have to be, the bound alone decides.
A program may use at most 384 MiB of HBM per device.

```python
import math
import jax
import jax.numpy as jnp
from jax import lax

ENSEMBLE_SIZE = 128
CELLS_FIRST_AXIS = 128
CELLS_SECOND_AXIS = 128
CELLS_DEPTHWISE = 64
PIX_ROW = 512
STEPS = 2
YB = 16


def draw_pixel_cell(key, part):
    per_cell = PIX_ROW // CELLS_SECOND_AXIS
    columns = jnp.arange(PIX_ROW, dtype=jnp.int32)
    centre = columns // per_cell
    base = centre // YB * YB
    jitter = jax.random.randint(key, (CELLS_FIRST_AXIS, PIX_ROW), -2, 3, dtype=jnp.int32)
    return base[None, :] + jnp.clip(centre[None, :] - base[None, :] + jitter, 0, YB - 1)


def touch_ends(drawn, rng, low, largest):
    spot = [jax.random.randint(jax.random.fold_in(rng, axis), (), 0, length) for axis, length in enumerate(drawn.shape)]
    longest = drawn.shape.index(max(drawn.shape))
    next_to = spot[:longest] + [(spot[longest] + 1) % drawn.shape[longest]] + spot[longest + 1:]
    return drawn.at[tuple(spot)].set(low).at[tuple(next_to)].set(largest)


def block_scale(rng, extent, cuts, low, high):
    def one(axis_at, blocks):
        steps = jax.random.uniform(jax.random.fold_in(jax.random.fold_in(rng, 6), axis_at), (blocks,), jnp.float32, low / len(cuts), high / len(cuts))
        return jnp.repeat(jnp.exp(steps), extent[axis_at] // blocks).reshape((-1,) + (1,) * (len(extent) - axis_at - 1))

    factor_of = one(*cuts[0])
    for cut in cuts[1:]:
        factor_of = factor_of * one(*cut)
    return factor_of


def bell_draw(stream_key, dims, spread, most, split=(), kind=jnp.bfloat16):
    result = spread * jax.random.normal(stream_key, dims, jnp.float32)
    if split:
        result = result * block_scale(stream_key, dims, split, -0.22, 0.18)
    return jnp.clip(result, -most, most).astype(kind)


def setup_inputs(seed: int = 0) -> dict:
    keys = jax.random.split(jax.random.key(seed), 8)
    return {
        "initial_heat_matrix": bell_draw(keys[0], (ENSEMBLE_SIZE, CELLS_FIRST_AXIS, CELLS_SECOND_AXIS * CELLS_DEPTHWISE), 1.0, 6.0, ((0, 8), (1, 4)), jnp.float32),
        "conductivity": jnp.clip(jnp.exp(math.log(2.0) - 1.3862944 * jax.random.uniform(keys[1], (CELLS_FIRST_AXIS, CELLS_SECOND_AXIS * CELLS_DEPTHWISE), jnp.float32) ** block_scale(keys[1], (CELLS_FIRST_AXIS, CELLS_SECOND_AXIS * CELLS_DEPTHWISE), ((0, 4),), -0.2, 0.2)), 0.5, 2.0),
        "laser_x": touch_ends(jax.random.randint(keys[2], (ENSEMBLE_SIZE, STEPS), 0, CELLS_FIRST_AXIS), jax.random.fold_in(keys[2], 1), 0, CELLS_FIRST_AXIS - 1).astype(jnp.int32),
        "laser_y": touch_ends(jax.random.randint(keys[3], (ENSEMBLE_SIZE, STEPS), 0, CELLS_SECOND_AXIS), jax.random.fold_in(keys[3], 1), 0, CELLS_SECOND_AXIS - 1).astype(jnp.int32),
        "pixel_cell": draw_pixel_cell(jax.random.fold_in(keys[7], 71), 0),
        "observed": bell_draw(keys[5], (CELLS_FIRST_AXIS, PIX_ROW), 1.0, 6.0, ((0, 4), (1, 8)), jnp.float32),
        "obs_var": jnp.clip(jnp.exp(math.log(400.0) - 2.9957323 * jax.random.uniform(keys[6], (CELLS_FIRST_AXIS, PIX_ROW), jnp.float32) ** block_scale(keys[6], (CELLS_FIRST_AXIS, PIX_ROW), ((0, 4), (1, 8)), -0.2, 0.2)), 20.0, 400.0),
    }


step_dt = 0.025
alpha_cond = 0.05
laser_power = 12.0
beam_spot_width = 18.0

def conduct(field_ext, cond_ext, first_plane, spot_x, spot_y):
    kext = cond_ext[None] * (1.0 + alpha_cond * field_ext * field_ext)
    fpad = jnp.pad(field_ext, ((0, 0), (0, 0), (1, 1), (1, 1)))
    kpad = jnp.pad(kext, ((0, 0), (0, 0), (1, 1), (1, 1)))
    centre = fpad[:, 1:-1, 1:-1, 1:-1]
    kcentre = kpad[:, 1:-1, 1:-1, 1:-1]
    shifted = [(slice(2, None), slice(1, -1), slice(1, -1)), (slice(None, -2), slice(1, -1), slice(1, -1)), (slice(1, -1), slice(2, None), slice(1, -1)), (slice(1, -1), slice(None, -2), slice(1, -1)), (slice(1, -1), slice(1, -1), slice(2, None)), (slice(1, -1), slice(1, -1), slice(None, -2))]
    flux = jnp.zeros_like(centre)
    for pick in shifted:
        neighbour = fpad[(slice(None),) + pick]
        kneigh = kpad[(slice(None),) + pick]
        flux = flux + 0.5 * (kcentre + kneigh) * (neighbour - centre)
    width = centre.shape[1]
    rows_y = centre.shape[2]
    depth = centre.shape[3]
    xglob = first_plane + jnp.arange(width, dtype=jnp.int32)
    yglob = jnp.arange(rows_y, dtype=jnp.int32)
    delta_x = (xglob[None, :] - spot_x[:, None]).astype(centre.dtype)
    delta_y = (yglob[None, :] - spot_y[:, None]).astype(centre.dtype)
    spot = laser_power * jnp.exp(-(delta_x[:, :, None] ** 2 + delta_y[:, None, :] ** 2) / beam_spot_width)
    surface_top = (jnp.arange(depth, dtype=jnp.int32) == depth - 1).astype(centre.dtype)
    heat = spot[:, :, :, None] * surface_top[None, None, None, :]
    return centre + step_dt * (flux + heat)

def reference(initial_heat_matrix, conductivity, laser_x, laser_y, pixel_cell, observed, obs_var):
    realization_batch = math.gcd(ENSEMBLE_SIZE, 8)
    thermal_profiles = initial_heat_matrix.reshape(ENSEMBLE_SIZE // realization_batch, realization_batch, CELLS_FIRST_AXIS, CELLS_SECOND_AXIS, CELLS_DEPTHWISE)
    cond_grid = conductivity.reshape(CELLS_FIRST_AXIS, CELLS_SECOND_AXIS, CELLS_DEPTHWISE)
    cond_ext = jnp.pad(cond_grid, ((1, 1), (0, 0), (0, 0)))
    heating_centres_first = laser_x.reshape(ENSEMBLE_SIZE // realization_batch, realization_batch, STEPS)
    heating_centres_second = laser_y.reshape(ENSEMBLE_SIZE // realization_batch, realization_batch, STEPS)

    def predicted_ensemble(flattened_ensemble):
        field, sx, sy = flattened_ensemble
        for tstep in range(STEPS):
            ext = jnp.pad(field, ((0, 0), (1, 1), (0, 0), (0, 0)))
            field = conduct(ext, cond_ext, jnp.int32(0), sx[:, tstep], sy[:, tstep])
        return field
    assimilated_outcome = lax.map(predicted_ensemble, (thermal_profiles, heating_centres_first, heating_centres_second))
    assimilated_outcome = assimilated_outcome.reshape(ENSEMBLE_SIZE, CELLS_FIRST_AXIS, CELLS_SECOND_AXIS, CELLS_DEPTHWISE)
    surface = assimilated_outcome[:, :, :, CELLS_DEPTHWISE - 1]
    index = jnp.broadcast_to(pixel_cell[None], (ENSEMBLE_SIZE, CELLS_FIRST_AXIS, PIX_ROW)).astype(jnp.int32)
    seen = jnp.take_along_axis(surface, index, axis=2)
    seen_mean = jnp.mean(seen, axis=0)
    seen_anom = seen - seen_mean[None]
    innovation = observed - seen_mean
    weight = 1.0 / obs_var
    gram = jnp.einsum('kxj,lxj->kl', seen_anom * weight[None], seen_anom, precision=lax.Precision.HIGHEST)
    proj = jnp.einsum('kxj,xj->k', seen_anom, weight * innovation, precision=lax.Precision.HIGHEST)
    eye = jnp.eye(ENSEMBLE_SIZE, dtype=gram.dtype)
    amat = eye + gram / (ENSEMBLE_SIZE - 1)
    chol = jnp.linalg.cholesky(amat)
    wroot = jax.scipy.linalg.solve_triangular(chol.T, eye, lower=False)
    middle = jax.scipy.linalg.solve_triangular(chol, proj[:, None], lower=True)
    wmean = jax.scipy.linalg.solve_triangular(chol.T, middle, lower=False)[:, 0] / (ENSEMBLE_SIZE - 1)
    mix = wroot + wmean[:, None]
    flat = assimilated_outcome.reshape(ENSEMBLE_SIZE, CELLS_FIRST_AXIS, CELLS_SECOND_AXIS * CELLS_DEPTHWISE)

    def transform(plane):
        fmean = jnp.mean(plane, axis=0)
        anom = plane - fmean[None]
        return fmean[None] + jnp.dot(mix.T, anom, precision=lax.Precision.HIGHEST)
    planes = lax.map(transform, jnp.transpose(flat, (1, 0, 2)))
    return jnp.transpose(planes, (1, 0, 2))
```

```python
import jax
import jax.numpy as jnp
from jax import lax
from jax.experimental import pallas as pl
from jax.experimental.pallas import tpu as pltpu
from jax.sharding import PartitionSpec as P

CELLS_DEPTHWISE = 64


step_dt = 0.025
alpha_cond = 0.05
laser_power = 12.0
beam_spot_width = 18.0


def halo(block, axis, width):
    count = lax.axis_size(axis)
    forward = [(i, i + 1) for i in range(count - 1)]
    backward = [(target, source) for source, target in forward]
    dim = block.ndim - 2
    low = lax.ppermute(
        lax.slice_in_dim(block, block.shape[dim] - width, None, axis=dim), axis, forward
    )
    high = lax.ppermute(lax.slice_in_dim(block, 0, width, axis=dim), axis, backward)
    return low, high


def forecast_kernel(
    depth, planes, wide, total_planes, first_ref, lx_ref, ly_ref, u_ref, low_ref, high_ref,
    cond_ref, out_ref, ustart, umid
):
    member = pl.program_id(0)
    rows = ustart.shape[0]
    parts, _, _, per_part = out_ref.shape
    columns = parts * per_part
    edge = 128
    ustart[2 : 2 + planes, edge : edge + columns] = u_ref[0]
    ustart[0:2, edge : edge + columns] = low_ref[0]
    ustart[2 + planes : 4 + planes, edge : edge + columns] = high_ref[0]
    ustart[4 + planes : rows, edge : edge + columns] = jnp.zeros(
        (rows - 4 - planes, columns), jnp.float32
    )
    for buf in (ustart, umid):
        buf[:, 0:edge] = jnp.zeros((rows, edge), jnp.float32)
        buf[:, edge + columns :] = jnp.zeros((rows, edge), jnp.float32)
    xpos = first_ref[0] - 2 + lax.broadcasted_iota(jnp.int32, (rows, 1), 0)
    inside = jnp.where((xpos >= 0) & (xpos < total_planes), 1.0, 0.0)
    lane = lax.broadcasted_iota(jnp.int32, (1, wide), 1)
    zpos = lane % depth
    top = zpos == depth - 1
    bottom = zpos == 0
    span = wide + 2 * edge

    def advance(source, start, step):
        ext = source[:, pl.ds(start, span)]
        kext = cond_ref[:, pl.ds(start, span)] * (1.0 + alpha_cond * ext * ext)
        centre = ext[:, edge : edge + wide]
        kcentre = kext[:, edge : edge + wide]

        def lanes(value, shift):
            return pltpu.roll(value, shift % span, 1)[:, edge : edge + wide]

        def face(neighbour, kneigh):
            return (kcentre + kneigh) * (neighbour - centre)

        flux = face(lanes(ext, depth), lanes(kext, depth))
        flux += face(lanes(ext, -depth), lanes(kext, -depth))
        flux += face(pltpu.roll(centre, 1, 0), pltpu.roll(kcentre, 1, 0))
        flux += face(pltpu.roll(centre, rows - 1, 0), pltpu.roll(kcentre, rows - 1, 0))
        flux += face(
            jnp.where(bottom, 0.0, lanes(ext, 1)), jnp.where(bottom, 0.0, lanes(kext, 1))
        )
        flux += face(
            jnp.where(top, 0.0, lanes(ext, -1)), jnp.where(top, 0.0, lanes(kext, -1))
        )
        dx = (xpos - lx_ref[member, step]).astype(jnp.float32)
        dy = ((start + lane) // depth - ly_ref[member, step]).astype(jnp.float32)
        along_x = jnp.exp(-(dx * dx) / beam_spot_width)
        along_y = jnp.exp(-(dy * dy) / beam_spot_width) * (step_dt * laser_power)
        heat = along_x * jnp.where(top, along_y, 0.0)
        return centre + (0.5 * step_dt) * flux + heat

    @pl.loop(0, columns // wide)
    def _(chunk):
        start = pl.multiple_of(chunk * wide, wide)
        umid[:, pl.ds(start + edge, wide)] = advance(ustart, start, 0) * inside

    @pl.loop(0, parts)
    def _(part):
        for sub in range(per_part // wide):
            start = pl.multiple_of(part * per_part + sub * wide, wide)
            done = advance(umid, start, 1)
            out_ref[part, 0, :, sub * wide : (sub + 1) * wide] = done[2 : 2 + planes]


def forecast(field, cond, lx, ly, parts, depth):
    members, planes, columns = field.shape
    first = (lax.axis_index("sa") * planes).astype(jnp.int32).reshape(1)
    total_planes = planes * lax.axis_size("sa")
    low, high = halo(field, "sa", 2)
    cond_low, cond_high = halo(cond, "sa", 2)
    rows = -(-(planes + 4) // 8) * 8
    cond_wide = jnp.pad(
        jnp.concatenate([cond_low, cond, cond_high], axis=0),
        ((0, rows - planes - 4), (128, 128)),
    )
    per_part = columns // parts
    wide = 512 if per_part % 512 == 0 else per_part
    smem = pl.BlockSpec(memory_space=pltpu.SMEM)
    return pl.pallas_call(
        lambda *refs: forecast_kernel(depth, planes, wide, total_planes, *refs),
        grid=(members,),
        in_specs=[
            smem, smem, smem,
            pl.BlockSpec((1, planes, columns), lambda m: (m, 0, 0)),
            pl.BlockSpec((1, 2, columns), lambda m: (m, 0, 0)),
            pl.BlockSpec((1, 2, columns), lambda m: (m, 0, 0)),
            pl.BlockSpec(cond_wide.shape, lambda m: (0, 0)),
        ],
        out_specs=pl.BlockSpec((parts, 1, planes, per_part), lambda m: (0, m, 0, 0)),
        out_shape=jax.ShapeDtypeStruct((parts, members, planes, per_part), jnp.float32),
        scratch_shapes=[pltpu.VMEM((rows, columns + 256), jnp.float32)] * 2,
        name="forecast",
    )(first, lx, ly, field, low, high, cond_wide)


def mix_kernel(gram_ref, proj_ref, out_ref, left, inverse):
    count = gram_ref.shape[0]
    row = lax.broadcasted_iota(jnp.int32, (count, count), 0)
    col = lax.broadcasted_iota(jnp.int32, (count, count), 1)
    eye = jnp.where(row == col, 1.0, 0.0)
    left[...] = eye + gram_ref[...] / (count - 1)
    inverse[...] = eye

    @pl.loop(0, count)
    def _(j):
        whole = left[...]
        pivot_row = left[pl.ds(j, 1), :]
        column = jnp.sum(jnp.where(col == j, whole, 0.0), axis=1, keepdims=True)
        pivot = jnp.sum(jnp.where(col[0:1] == j, pivot_row, 0.0), axis=1, keepdims=True)
        scale = 1.0 / jnp.sqrt(pivot)
        fresh = inverse[pl.ds(j, 1), :] * scale
        below = jnp.where(row[:, 0:1] > j, column * scale, 0.0)
        left[...] = whole - below * (pivot_row * scale)
        inverse[...] = jnp.where(row == j, fresh, inverse[...] - below * fresh)

    root = inverse[...]
    solved = jnp.sum(root * proj_ref[...], axis=1, keepdims=True)
    wmean = jnp.sum(root * solved, axis=0, keepdims=True) / (count - 1)
    mix = root + wmean
    out_ref[...] = mix + (1.0 - jnp.sum(mix, axis=1, keepdims=True)) / count


def join_kernel(parts_ref, out_ref):
    parts, _, _, per_part = parts_ref.shape
    for part in range(parts):
        out_ref[0, :, part * per_part : (part + 1) * per_part] = parts_ref[part, 0]


def per_device(initial_heat_matrix, conductivity, laser_x, laser_y, pixel_cell, observed, obs_var):
    members, planes, columns = initial_heat_matrix.shape
    depth = CELLS_DEPTHWISE
    parts = lax.axis_size("ma")
    per_part = columns // parts
    total_members = members * parts
    states = forecast(initial_heat_matrix, conductivity, laser_x, laser_y, parts, depth)
    gathered = lax.all_to_all(
        states.reshape(total_members, planes, per_part), "ma", split_axis=0, concat_axis=0, tiled=True
    )
    group_rows = per_part // depth
    surface = lax.slice(
        gathered, (0, 0, depth - 1), gathered.shape, (1, 1, depth)
    )
    local_rows = pixel_cell % group_rows
    onehot = (
        local_rows[:, None, :] == jnp.arange(group_rows, dtype=jnp.int32)[None, :, None]
    ).astype(jnp.float32)
    seen = jnp.einsum("kxy,xyj->kxj", surface, onehot, precision=lax.Precision.HIGHEST)
    seen_mean = jnp.mean(seen, axis=0)
    seen_anom = seen - seen_mean[None]
    innovation = observed - seen_mean
    weight = 1.0 / obs_var
    gram_part = jnp.einsum(
        "kxj,lxj->kl", seen_anom * weight[None], seen_anom, precision=lax.Precision.HIGHEST
    )
    proj_part = jnp.einsum(
        "kxj,xj->k", seen_anom, weight * innovation, precision=lax.Precision.HIGHEST
    )
    gram, proj = lax.psum((gram_part, proj_part), ("ma", "sa"))
    mix = pl.pallas_call(
        mix_kernel,
        out_shape=jax.ShapeDtypeStruct(gram.shape, jnp.float32),
        scratch_shapes=[pltpu.VMEM(gram.shape, jnp.float32)] * 2,
        name="mix",
    )(gram, proj.reshape(1, total_members))
    done = jnp.einsum("jxc,kj->kxc", gathered, mix, precision=lax.Precision.HIGHEST)
    back = lax.all_to_all(done, "ma", split_axis=0, concat_axis=0, tiled=True)
    return pl.pallas_call(
        join_kernel,
        grid=(members,),
        in_specs=[pl.BlockSpec((parts, 1, planes, per_part), lambda m: (0, m, 0, 0))],
        out_specs=pl.BlockSpec((1, planes, columns), lambda m: (m, 0, 0)),
        out_shape=jax.ShapeDtypeStruct((members, planes, columns), jnp.float32),
        name="join",
    )(back.reshape(parts, members, planes, per_part))


def solution(mesh):
    placed = (
        P("ma", "sa", None),
        P("sa", None),
        P("ma", None),
        P("ma", None),
        P("sa", "ma"),
        P("sa", "ma"),
        P("sa", "ma"),
    )
    return jax.shard_map(
        per_device, mesh=mesh, in_specs=placed, out_specs=P("ma", "sa", None), check_vma=False
    )
```
